512 devices in a mesh: tm: 128 (over z, y, core), batch: 4 (over x).
Axes of the slice: x: 4, y: 4, z: 16, core: 2. Of those that a mesh axis runs over, the one named last changes fastest.
Arguments:
- inputs: bfloat16 [4096, 4, 128], P('tm', 'batch'), may hold values from -6 to 6
- h_start: float32 [4, 128], P('batch'), may hold values from -4 to 4
- in_weight: bfloat16 [128, 384], replicated, may hold values from -0.5 to 0.5
- rec_weight: float32 [128, 384], replicated, may hold values from -0.5 to 0.5
- update_bias: float32 [128], replicated, may hold values from -1 to 14
- reset_bias: float32 [128], replicated, may hold values from -4 to 4
- cand_bias: float32 [128], replicated, may hold values from -3 to 3
- rec_bias: float32 [128], replicated, may hold values from -3 to 3
Outputs:
- states: float32 [4096, 4, 128], P('tm', 'batch')
- residual_norms: float32 [2], replicated
The draws below stay inside these ranges and needn't reach their ends.
All inputs are finite; a program needn't handle non-finite values.
Results may differ from the reference program's by a relative error of at most 0.0003.
Values sent between devices are 32-bit elements; how exact they have to be, the bound alone decides.
A program may use at most 64 MiB of HBM per device.

```python
import math
import jax
import jax.numpy as jnp
from jax import lax

H = 128
DIN = 128
STEPS_DEV = 32
ITERS = 2
BATCH = 4
TOTAL = 4096


def draw_update_bias(key, part):
    key_pick = jax.random.fold_in(key, 11)
    key_slow = jax.random.fold_in(key, 12)
    key_fast = jax.random.fold_in(key, 13)
    key_middle = jax.random.fold_in(key, 14)
    slow_cut = 7
    middle_cut = 14
    kinds = jax.random.randint(key_pick, (H,), 0, 20)
    slow_bias = math.log(TOTAL) + jax.random.uniform(key_slow, (H,), jnp.float32, -0.5, 1.0)
    middle_bias = math.log(STEPS_DEV) + jax.random.uniform(key_middle, (H,), jnp.float32, 0.0, 2.5)
    fast_bias = jax.random.uniform(key_fast, (H,), jnp.float32, -1.0, 3.0)
    chosen = jnp.where(kinds < slow_cut, slow_bias, jnp.where(kinds < middle_cut, middle_bias, fast_bias))
    return chosen.astype(jnp.float32)


def levels(own_key, dims, shards, least, high):
    gain, own = 1.0, jax.random.fold_in(own_key, 6)
    for dim, shards_of in shards:
        heights = jnp.exp(jax.random.uniform(jax.random.fold_in(own, dim), (shards_of,), jnp.float32, least / len(shards), high / len(shards)))
        gain = gain * jnp.repeat(heights, dims[dim] // shards_of).reshape([-1 if axis == dim else 1 for axis in range(len(dims))])
    return gain


def gaussian(stream_key, shape, scale, most, cuts=(), kind=jnp.bfloat16):
    result = jax.random.normal(stream_key, shape, jnp.float32) * scale
    if len(cuts) > 0:
        result = levels(stream_key, shape, cuts, -0.22, 0.18) * result
    return jnp.clip(result, min=-most, max=most).astype(kind)


def setup_inputs(seed: int = 0) -> dict:
    keys = jax.random.split(jax.random.key(seed), 9)
    inputs = gaussian(keys[0], (TOTAL, BATCH, DIN), 1.0, 6.0, ((0, 128), (1, 4)))
    h_start = gaussian(keys[1], (BATCH, H), 0.5, 4.0, ((0, 4),), jnp.float32)
    in_weight = gaussian(keys[2], (DIN, 3 * H), DIN ** -0.5, 0.5)
    rec_weight = gaussian(keys[3], (H, 3 * H), H ** -0.5, 0.5, (), jnp.float32)
    update_bias = draw_update_bias(jax.random.fold_in(keys[8], 71), 0)
    reset_bias = gaussian(keys[5], (H,), 1.0, 4.0, (), jnp.float32)
    cand_bias = gaussian(keys[6], (H,), 0.5, 3.0, (), jnp.float32)
    rec_bias = gaussian(keys[7], (H,), 0.5, 3.0, (), jnp.float32)
    return {"inputs": inputs, "h_start": h_start, "in_weight": in_weight, "rec_weight": rec_weight, "update_bias": update_bias, "reset_bias": reset_bias, "cand_bias": cand_bias, "rec_bias": rec_bias}


HIGH = lax.Precision.HIGHEST

def cell_parts(in_gates, previous, rec_weight, update_bias, reset_bias, cand_bias, rec_bias):
    units = rec_weight.shape[0]
    rec_gates = jnp.dot(previous, rec_weight, precision=HIGH)
    update_gate = jax.nn.sigmoid(in_gates[:, :units] + rec_gates[:, :units] + update_bias)
    reset_gate = jax.nn.sigmoid(in_gates[:, units:2 * units] + rec_gates[:, units:2 * units] + reset_bias)
    recur_term = rec_gates[:, 2 * units:] + rec_bias
    candidate = jnp.tanh(in_gates[:, 2 * units:] + cand_bias + reset_gate * recur_term)
    stepped = (1.0 - update_gate) * candidate + update_gate * previous
    return (update_gate, reset_gate, recur_term, candidate, stepped)

def jacobian(previous, update_gate, reset_gate, recur_term, candidate, rec_weight, identity):
    units = rec_weight.shape[0]
    coef_update = (previous - candidate) * update_gate * (1.0 - update_gate)
    common = (1.0 - update_gate) * (1.0 - candidate * candidate)
    coef_cand = common * reset_gate
    coef_reset = common * recur_term * reset_gate * (1.0 - reset_gate)
    return identity * update_gate[..., None, :] + rec_weight[:, :units] * coef_update[..., None, :] + rec_weight[:, units:2 * units] * coef_reset[..., None, :] + rec_weight[:, 2 * units:] * coef_cand[..., None, :]

def reference(inputs, h_start, in_weight, rec_weight, update_bias, reset_bias, cand_bias, rec_bias):
    units = rec_weight.shape[0]
    identity = jnp.eye(units, dtype=jnp.float32)
    weights = (jnp.arange(TOTAL).astype(jnp.float32) + 1.0) / TOTAL
    sums = [jnp.zeros((), jnp.float32) for newton in range(ITERS)]
    results = []
    for sequence in range(BATCH):
        in_gates = jnp.dot(inputs[:, sequence, :], in_weight, preferred_element_type=jnp.float32)
        start = h_start[sequence]
        previous = jnp.zeros((TOTAL, units), jnp.float32).at[0].set(start)
        current = previous
        for newton in range(ITERS):
            parts = cell_parts(in_gates, previous, rec_weight, update_bias, reset_bias, cand_bias, rec_bias)
            if newton > 0:
                sums[newton - 1] = sums[newton - 1] + jnp.sum(weights[:, None] * (current - parts[4]) ** 2)

            def advance(carried, item):
                prev_row, gate_z, gate_r, recur_row, cand_row, step_row = item
                matrix = jacobian(prev_row, gate_z, gate_r, recur_row, cand_row, rec_weight, identity)
                offset = step_row - jnp.dot(prev_row, matrix, precision=HIGH)
                carried = jnp.dot(carried, matrix, precision=HIGH) + offset
                return (carried, carried)
            final_row, current = lax.scan(advance, start, (previous,) + tuple(parts))
            previous = jnp.concatenate([start[None, :], current[:-1]], axis=0)
        parts = cell_parts(in_gates, previous, rec_weight, update_bias, reset_bias, cand_bias, rec_bias)
        sums[ITERS - 1] = sums[ITERS - 1] + jnp.sum(weights[:, None] * (current - parts[4]) ** 2)
        results.append(current)
    states = jnp.stack(results, axis=1)
    denom = BATCH * units * (TOTAL + 1) / 2.0
    residual_norms = jnp.sqrt(jnp.stack(sums) / denom + 1e-06)
    return (states, residual_norms)
```

```python
import functools
import jax
import jax.numpy as jnp
from jax import lax
from jax.experimental import pallas as pl
from jax.experimental.pallas import tpu as pltpu
from jax.sharding import PartitionSpec as P

ITERS = 2
BLOCKS = 4
PLANE = 8
ZROUNDS = 1
H = 128
ROWS = H + 8
F32 = jnp.float32
BF16 = jnp.bfloat16


def split(value):
    high = value.astype(BF16)
    low = (value - high.astype(F32)).astype(BF16)
    return high, low


def split_dot(left, right):
    left_high, left_low = split(left)
    right_high, right_low = split(right)
    width = right.shape[1]
    both = jnp.concatenate([right_high, right_low], axis=1)
    out = jnp.dot(
        jnp.concatenate([left_high, left_low], axis=1),
        jnp.concatenate([both, both], axis=0),
        preferred_element_type=F32,
    )
    return out[:, :width] + out[:, width:]


def compose(early, late):
    return early + late + split_dot(early, late[:H])


def kernel(
    nz, nx,
    x_ref, start_ref, in_w_ref, rec_w_ref, ub_ref, rb_ref, cb_ref, nb_ref,
    out_ref, norm_ref,
    gx, coef, offs, prefix, own, got, acc, zown, zgot, hvec, hgot, hbuf, heads,
    part_a, part_b, part_c,
    m_send, m_recv, z_send, z_recv, h_send, h_recv,
    a_send, a_recv, b_send, b_recv, c_send, c_recv,
):
    steps = x_ref.shape[0]
    length = steps // BLOCKS
    me = lax.axis_index("tm")
    col = lax.axis_index("batch")
    z = me // PLANE
    inner = me % PLANE
    y = inner // 2
    core = inner % 2

    mates = (
        z * PLANE + y * 2 + (1 - core),
        z * PLANE + (y + 1 - 2 * (y % 2)) * 2 + core,
        z * PLANE + (3 - y) * 2 + core,
    )
    uppers = (core == 1, y % 2 == 1, y >= 2)

    barrier = pltpu.get_barrier_semaphore()

    def hello(**where):
        pl.semaphore_signal(
            barrier, inc=1, device_id=where, device_id_type=pl.DeviceIdType.MESH
        )

    for j in range(1, PLANE):
        hello(tm=z * PLANE + (inner + j) % PLANE)
    for j in range(1, nz):
        hello(tm=((z + j) % nz) * PLANE + inner)
    for j in range(1, nx):
        hello(batch=(col + j) % nx)

    eye = (
        lax.broadcasted_iota(jnp.int32, (H, H), 0)
        == lax.broadcasted_iota(jnp.int32, (H, H), 1)
    ).astype(F32)

    def apply(row, mapped):
        column = jnp.sum(eye * row[:1], axis=1, keepdims=True)
        moved = jnp.sum(column * mapped[:H], axis=0, keepdims=True)
        return row + jnp.broadcast_to(moved + mapped[H : H + 1], row.shape)

    def push(src, dst, ssem, rsem, **where):
        return pltpu.make_async_remote_copy(
            src_ref=src, dst_ref=dst, send_sem=ssem, recv_sem=rsem,
            device_id=where, device_id_type=pl.DeviceIdType.MESH,
        )

    gx[...] = jnp.dot(x_ref[...], in_w_ref[...], preferred_element_type=F32)
    start = jnp.broadcast_to(start_ref[...], (8, H))
    weight = (
        (me * steps + lax.broadcasted_iota(jnp.int32, (steps, 1), 0)).astype(F32) + 1.0
    ) / (steps * nz * PLANE)

    def cell(prev):
        gh = split_dot(prev, rec_w_ref[...])
        update = jax.nn.sigmoid(gx[:, :H] + gh[:, :H] + ub_ref[...])
        reset = jax.nn.sigmoid(gx[:, H : 2 * H] + gh[:, H : 2 * H] + rb_ref[...])
        recur = gh[:, 2 * H :] + nb_ref[...]
        cand = jnp.tanh(gx[:, 2 * H :] + cb_ref[...] + reset * recur)
        stepped = (1.0 - update) * cand + update * prev
        return gh, update, reset, recur, cand, stepped

    first = jnp.where(me == 0, start_ref[...], jnp.zeros((1, H), F32))
    prev = jnp.where(
        lax.broadcasted_iota(jnp.int32, (steps, H), 0) == 0,
        jnp.broadcast_to(first, (steps, H)),
        jnp.zeros((steps, H), F32),
    )
    current = prev
    sums = []

    for it in range(ITERS):
        gh, update, reset, recur, cand, stepped = cell(prev)
        if it > 0:
            sums.append(
                jnp.sum(weight * (current - stepped) ** 2, axis=0, keepdims=True)
            )
        c_update = (prev - cand) * update * (1.0 - update)
        common = (1.0 - update) * (1.0 - cand * cand)
        c_cand = common * reset
        c_reset = common * recur * reset * (1.0 - reset)
        coef[0] = c_update
        coef[1] = c_reset
        coef[2] = c_cand
        coef[3] = update - 1.0
        offs[...] = stepped - (
            update * prev
            + c_update * gh[:, :H]
            + c_reset * gh[:, H : 2 * H]
            + c_cand * gh[:, 2 * H :]
        )

        def step_matrix(t):
            at = pl.ds(t, 1)
            return (
                rec_w_ref[:, :H] * coef[0, at, :]
                + rec_w_ref[:, H : 2 * H] * coef[1, at, :]
                + rec_w_ref[:, 2 * H :] * coef[2, at, :]
                + eye * coef[3, at, :]
            )

        pad_row = lax.broadcasted_iota(jnp.int32, (8, H), 0) == 0

        def step_tail(t):
            return jnp.where(
                pad_row, jnp.broadcast_to(offs[pl.ds(t, 1), :], (8, H)), 0.0
            )

        for b in range(BLOCKS):
            prefix[b, 0, :H] = step_matrix(b * length)
            prefix[b, 0, H:] = step_tail(b * length)

        def extend(t, carry):
            for b in range(BLOCKS):
                before = prefix[b, t - 1]
                late = step_matrix(b * length + t)
                more = split_dot(before, late)
                prefix[b, t, :H] = before[:H] + late + more[:H]
                prefix[b, t, H:] = before[H:] + step_tail(b * length + t) + more[H:]
            return carry

        lax.fori_loop(1, length, extend, 0)

        last = length - 1
        heads[1] = prefix[0, last]
        heads[2] = compose(prefix[0, last], prefix[1, last])
        tail_pair = compose(prefix[2, last], prefix[3, last])
        own[it, 0] = compose(heads[2], tail_pair)

        if it == 0:
            pl.semaphore_wait(barrier, (PLANE - 1) + (nz - 1) + (nx - 1))

        copies = []
        for k in range(3):
            copy = push(
                own.at[it, k], got.at[it, k], m_send.at[it, k], m_recv.at[it, k],
                tm=mates[k],
            )
            copy.start()
            copies.append(copy)
            if k == 0:
                heads[3] = compose(heads[2], prefix[2, last])
            copy.wait_recv()
            mine = own[it, k]
            theirs = got[it, k]
            early = jnp.where(uppers[k], theirs, mine)
            late = jnp.where(uppers[k], mine, theirs)
            merged = compose(early, late)
            if k < 2:
                own[it, k + 1] = merged
            else:
                zown[it, 0] = merged

        h_copy_out = []

        def relay(to, level, valid):
            @pl.when(valid)
            def _():
                hvec[it, 1 + level] = apply(hvec[it, 0], zown[it, level])
                push(
                    hvec.at[it, 1 + level], hgot.at[it],
                    h_send.at[it, level], h_recv.at[it],
                    tm=jnp.minimum(z + to, nz - 1) * PLANE + inner,
                ).start()
            h_copy_out.append((to, level, valid))

        def receive(valid):
            @pl.when(valid)
            def _():
                push(
                    hgot.at[it], hgot.at[it], h_send.at[it, 0], h_recv.at[it],
                    tm=me,
                ).wait_recv()
                hvec[it, 0] = hgot[it]

        @pl.when(z == 0)
        def _():
            hvec[it, 0] = start

        z_out = []
        for k in range(ZROUNDS):
            d = 1 << k

            @pl.when(z >= d)
            def _():
                push(
                    zown.at[it, k], zgot.at[it, k], z_send.at[it, k], z_recv.at[it, k],
                    tm=(jnp.maximum(z - d, 0)) * PLANE + inner,
                ).start()

            z_out.append(d)
            if k > 0:
                receive((z >= d // 2) & (z < d))
            relay(d, k, z < d)

            @pl.when(z + d < nz)
            def _():
                push(
                    zown.at[it, k], zgot.at[it, k], z_send.at[it, k], z_recv.at[it, k],
                    tm=me,
                ).wait_recv()
                zown[it, k + 1] = compose(zown[it, k], zgot[it, k])

        wide = 1 << ZROUNDS
        known = 1 if ZROUNDS == 0 else wide // 2

        zero = jnp.zeros((ROWS, H), F32)

        def inner_map():
            lead = jnp.where(uppers[2], got[it, 2], zero)
            acc[0] = compose(lead, jnp.where(uppers[1], got[it, 1], zero))
            acc[1] = compose(acc[0], jnp.where(uppers[0], got[it, 0], zero))
            for b in range(1, BLOCKS):
                acc[1 + b] = compose(acc[1], heads[b])

        @pl.when(z < known)
        def _():
            @pl.when(z + wide < nz)
            def _():
                hvec[it, 1 + ZROUNDS] = apply(hvec[it, 0], zown[it, ZROUNDS])
                push(
                    hvec.at[it, 1 + ZROUNDS], hgot.at[it],
                    h_send.at[it, ZROUNDS], h_recv.at[it],
                    tm=jnp.minimum(z + wide, nz - 1) * PLANE + inner,
                ).start()

        inner_map()
        receive(z >= known)
        relay(wide, ZROUNDS, (z >= known) & (z + wide < nz))

        entering = hvec[it, 0]
        at_device = apply(entering, acc[1])
        hbuf[0:8] = at_device
        for b in range(BLOCKS):
            head = at_device if b == 0 else apply(entering, acc[1 + b])
            column = jnp.sum(eye * head[:1], axis=1, keepdims=True)
            rows = []
            for t in range(length):
                moved = jnp.sum(column * prefix[b, t, :H], axis=0, keepdims=True)
                rows.append(moved + prefix[b, t, H : H + 1] + head[:1])
            hbuf[8 + b * length : 8 + (b + 1) * length] = jnp.concatenate(rows, axis=0)
        current = hbuf[8 : 8 + steps]
        prev = hbuf[7 : 7 + steps]

        for k in range(3):
            copies[k].wait_send()
        for k, d in enumerate(z_out):
            @pl.when(z >= d)
            def _():
                push(
                    zown.at[it, k], zgot.at[it, k], z_send.at[it, k], z_recv.at[it, k],
                    tm=me,
                ).wait_send()
        for level in range(ZROUNDS + 1):
            d = 1 << level
            sent = (z + wide < nz) if level == ZROUNDS else (z < d)

            @pl.when(sent)
            def _():
                push(
                    hvec.at[it, 1 + level], hgot.at[it],
                    h_send.at[it, level], h_recv.at[it],
                    tm=me,
                ).wait_send()

    out_ref[...] = current
    stepped = cell(prev)[5]
    sums.append(jnp.sum(weight * (current - stepped) ** 2, axis=0, keepdims=True))
    total = jnp.concatenate(sums + [jnp.zeros((8 - ITERS, H), F32)], axis=0)

    def exchange(total, part, send, recv, mine, peers, place):
        part[mine] = total
        sent = []
        for j in range(1, peers):
            copy = push(
                part.at[mine], part.at[mine], send.at[j], recv.at[mine],
                **place((mine + j) % peers),
            )
            copy.start()
            sent.append(copy)
        for j in range(1, peers):
            other = (mine + j) % peers
            push(
                part.at[other], part.at[other], send.at[j], recv.at[other],
                **place(other),
            ).wait_recv()
        for copy in sent:
            copy.wait_send()
        total = part[0]
        for j in range(1, peers):
            total = total + part[j]
        return total

    total = exchange(
        total, part_a, a_send, a_recv, inner, PLANE,
        lambda other: {"tm": z * PLANE + other},
    )
    total = exchange(
        total, part_b, b_send, b_recv, col, nx, lambda other: {"batch": other}
    )
    total = exchange(
        total, part_c, c_send, c_recv, z, nz,
        lambda other: {"tm": other * PLANE + inner},
    )
    denom = nx * H * (steps * nz * PLANE + 1) / 2.0
    norms = jnp.sqrt(jnp.sum(total, axis=1, keepdims=True) / denom + 1e-06)
    for k in range(ITERS):
        norm_ref[k] = norms[k, 0]


def per_device(
    nz, nx, inputs, h_start, in_weight, rec_weight, update_bias, reset_bias,
    cand_bias, rec_bias,
):
    steps = inputs.shape[0]
    length = steps // BLOCKS
    vmem = pl.BlockSpec(memory_space=pltpu.VMEM)
    dma = pltpu.SemaphoreType.DMA
    states, norms = pl.pallas_call(
        functools.partial(kernel, nz, nx),
        out_shape=(
            jax.ShapeDtypeStruct((steps, H), F32),
            jax.ShapeDtypeStruct((ITERS,), F32),
        ),
        in_specs=[vmem] * 8,
        out_specs=(vmem, pl.BlockSpec(memory_space=pltpu.SMEM)),
        scratch_shapes=[
            pltpu.VMEM((steps, 3 * H), F32),
            pltpu.VMEM((4, steps, H), F32),
            pltpu.VMEM((steps, H), F32),
            pltpu.VMEM((BLOCKS, length, ROWS, H), F32),
            pltpu.VMEM((ITERS, 3, ROWS, H), F32),
            pltpu.VMEM((ITERS, 3, ROWS, H), F32),
            pltpu.VMEM((1 + BLOCKS, ROWS, H), F32),
            pltpu.VMEM((ITERS, ZROUNDS + 1, ROWS, H), F32),
            pltpu.VMEM((ITERS, max(ZROUNDS, 1), ROWS, H), F32),
            pltpu.VMEM((ITERS, ZROUNDS + 2, 8, H), F32),
            pltpu.VMEM((ITERS, 8, H), F32),
            pltpu.VMEM((8 + steps, H), F32),
            pltpu.VMEM((BLOCKS, ROWS, H), F32),
            pltpu.VMEM((PLANE, 8, H), F32),
            pltpu.VMEM((nx, 8, H), F32),
            pltpu.VMEM((nz, 8, H), F32),
            dma((ITERS, 3)), dma((ITERS, 3)),
            dma((ITERS, max(ZROUNDS, 1))), dma((ITERS, max(ZROUNDS, 1))),
            dma((ITERS, ZROUNDS + 1)), dma((ITERS,)),
            dma((PLANE,)), dma((PLANE,)),
            dma((nx,)), dma((nx,)),
            dma((nz,)), dma((nz,)),
        ],
        compiler_params=pltpu.CompilerParams(collective_id=0, has_side_effects=True),
        name="deer",
    )(
        inputs.reshape(steps, -1), h_start, in_weight, rec_weight,
        update_bias.reshape(1, H), reset_bias.reshape(1, H),
        cand_bias.reshape(1, H), rec_bias.reshape(1, H),
    )
    return states.reshape(steps, 1, H), norms


def solution(mesh):
    nz = mesh.shape["tm"] // PLANE
    nx = mesh.shape["batch"]
    in_specs = (P("tm", "batch", None), P("batch", None), P(), P(), P(), P(), P(), P())
    out_specs = (P("tm", "batch", None), P())
    return jax.shard_map(
        functools.partial(per_device, nz, nx), mesh=mesh, in_specs=in_specs,
        out_specs=out_specs, check_vma=False,
    )
```

```python
import functools
import jax
import jax.numpy as jnp
from jax import lax
from jax.experimental import pallas as pl
from jax.experimental.pallas import tpu as pltpu
from jax.sharding import PartitionSpec as P

ITERS = 2
BLOCKS = 4
YS = 4
PLANE = 2 * YS
ZROUNDS = 1
H = 128
ROWS = H + 8
F32 = jnp.float32
BF16 = jnp.bfloat16


def split(value):
    high = value.astype(BF16)
    low = (value - high.astype(F32)).astype(BF16)
    return high, low


def split_dot(left, right):
    left_high, left_low = split(left)
    right_high, right_low = split(right)
    width = right.shape[1]
    both = jnp.concatenate([right_high, right_low], axis=1)
    out = jnp.dot(
        jnp.concatenate([left_high, left_low], axis=1),
        jnp.concatenate([both, both], axis=0),
        preferred_element_type=F32,
    )
    return out[:, :width] + out[:, width:]


def compose(early, late):
    return early + late + split_dot(early, late[:H])


def kernel(
    nz, nx,
    x_ref, start_ref, in_w_ref, rec_w_ref, ub_ref, rb_ref, cb_ref, nb_ref,
    out_ref, norm_ref,
    gx, coef, offs, prefix, own, got, chips, lead, acc, zown, zgot, hvec, hgot, hbuf,
    heads, part_a, part_b, part_c, reach,
    m_send, m_recv, y_send, y_recv, z_send, z_recv, h_send, h_recv,
    a_send, a_recv, b_send, b_recv, c_send, c_recv,
):
    steps = x_ref.shape[0]
    length = steps // BLOCKS
    me = lax.axis_index("tm")
    col = lax.axis_index("batch")
    z = me // PLANE
    inner = me % PLANE
    y = inner // 2
    core = inner % 2

    twin = z * PLANE + y * 2 + (1 - core)

    def along_y(j):
        return z * PLANE + ((y + j) % YS) * 2 + core

    def along_z(j):
        return ((z + j) % nz) * PLANE + inner

    others = sorted(
        ((j, i) for j in range(YS) for i in range(nx) if i or j),
        key=lambda ji: -min(ji[0], YS - ji[0]) - min(ji[1], nx - ji[1]),
    )
    far_z = sorted(range(1, nz), key=lambda j: -min(j, nz - j))

    barrier = pltpu.get_barrier_semaphore()

    def hello(sem, **where):
        pl.semaphore_signal(
            sem, inc=1, device_id=where, device_id_type=pl.DeviceIdType.MESH
        )

    near = [-2, -1, 1, 2]
    hello(barrier, tm=twin)
    for j in near:
        hello(barrier, tm=along_z(j))
    for j, i in others:
        hello(barrier, tm=along_y(j), batch=(col + i) % nx)

    eye = (
        lax.broadcasted_iota(jnp.int32, (H, H), 0)
        == lax.broadcasted_iota(jnp.int32, (H, H), 1)
    ).astype(F32)

    def apply(row, mapped):
        column = jnp.sum(eye * row[:1], axis=1, keepdims=True)
        moved = jnp.sum(column * mapped[:H], axis=0, keepdims=True)
        return row + jnp.broadcast_to(moved + mapped[H : H + 1], row.shape)

    def push(src, dst, ssem, rsem, **where):
        return pltpu.make_async_remote_copy(
            src_ref=src, dst_ref=dst, send_sem=ssem, recv_sem=rsem,
            device_id=where, device_id_type=pl.DeviceIdType.MESH,
        )

    gx[...] = jnp.dot(x_ref[...], in_w_ref[...], preferred_element_type=F32)
    start = jnp.broadcast_to(start_ref[...], (8, H))
    weight = (
        (me * steps + lax.broadcasted_iota(jnp.int32, (steps, 1), 0)).astype(F32) + 1.0
    ) / (steps * nz * PLANE)

    def cell(prev):
        gh = split_dot(prev, rec_w_ref[...])
        update = jax.nn.sigmoid(gx[:, :H] + gh[:, :H] + ub_ref[...])
        reset = jax.nn.sigmoid(gx[:, H : 2 * H] + gh[:, H : 2 * H] + rb_ref[...])
        recur = gh[:, 2 * H :] + nb_ref[...]
        cand = jnp.tanh(gx[:, 2 * H :] + cb_ref[...] + reset * recur)
        stepped = (1.0 - update) * cand + update * prev
        return gh, update, reset, recur, cand, stepped

    first = jnp.where(me == 0, start_ref[...], jnp.zeros((1, H), F32))
    prev = jnp.where(
        lax.broadcasted_iota(jnp.int32, (steps, H), 0) == 0,
        jnp.broadcast_to(first, (steps, H)),
        jnp.zeros((steps, H), F32),
    )
    current = prev
    sums = []

    for it in range(ITERS):
        gh, update, reset, recur, cand, stepped = cell(prev)
        if it > 0:
            sums.append(
                jnp.sum(weight * (current - stepped) ** 2, axis=0, keepdims=True)
            )
        c_update = (prev - cand) * update * (1.0 - update)
        common = (1.0 - update) * (1.0 - cand * cand)
        c_cand = common * reset
        c_reset = common * recur * reset * (1.0 - reset)
        coef[0] = c_update
        coef[1] = c_reset
        coef[2] = c_cand
        coef[3] = update - 1.0
        offs[...] = stepped - (
            update * prev
            + c_update * gh[:, :H]
            + c_reset * gh[:, H : 2 * H]
            + c_cand * gh[:, 2 * H :]
        )

        def step_matrix(t):
            at = pl.ds(t, 1)
            return (
                rec_w_ref[:, :H] * coef[0, at, :]
                + rec_w_ref[:, H : 2 * H] * coef[1, at, :]
                + rec_w_ref[:, 2 * H :] * coef[2, at, :]
                + eye * coef[3, at, :]
            )

        pad_row = lax.broadcasted_iota(jnp.int32, (8, H), 0) == 0

        def step_tail(t):
            return jnp.where(
                pad_row, jnp.broadcast_to(offs[pl.ds(t, 1), :], (8, H)), 0.0
            )

        for b in range(BLOCKS):
            prefix[b, 0, :H] = step_matrix(b * length)
            prefix[b, 0, H:] = step_tail(b * length)

        def extend(t, carry):
            before = [prefix[b, t - 1] for b in range(BLOCKS)]
            late = [step_matrix(b * length + t) for b in range(BLOCKS)]
            tail = [step_tail(b * length + t) for b in range(BLOCKS)]
            more = [split_dot(before[b], late[b]) for b in range(BLOCKS)]
            for b in range(BLOCKS):
                prefix[b, t, :H] = before[b][:H] + late[b] + more[b][:H]
                prefix[b, t, H:] = before[b][H:] + tail[b] + more[b][H:]
            return carry

        lax.fori_loop(1, length, extend, 0, unroll=True)

        last = length - 1
        ends = [prefix[b, last] for b in range(BLOCKS)]
        head_pair = compose(ends[0], ends[1])
        whole = compose(head_pair, compose(ends[2], ends[3]))
        own[it] = whole
        if it == 0:
            pl.semaphore_wait(barrier, 1 + len(near) + len(others))
            for j in (-2, 2):
                hello(reach.at[0], tm=along_z(j))
        pair_copy = push(own.at[it], got.at[it], m_send.at[it], m_recv.at[it], tm=twin)
        pair_copy.start()
        heads[0] = ends[0]
        heads[1] = head_pair
        heads[2] = compose(head_pair, ends[2])
        pair_copy.wait_recv()
        theirs = got[it]
        early = jnp.where(core == 1, theirs, whole)
        late = jnp.where(core == 1, whole, theirs)
        chips[it, y] = compose(early, late)
        chip_copies = []
        for j in (2, 1, 3):
            copy = push(
                chips.at[it, y], chips.at[it, y], y_send.at[it, j], y_recv.at[it, y],
                tm=along_y(j),
            )
            copy.start()
            chip_copies.append(copy)
        if it == 0:
            pl.semaphore_wait(reach.at[0], 2)
            for j in (-4, 4):
                hello(reach.at[1], tm=along_z(j))
        for j in (1, 3, 2):
            source = (y + j) % YS
            push(
                chips.at[it, source], chips.at[it, source],
                y_send.at[it, j], y_recv.at[it, source], tm=along_y(j),
            ).wait_recv()
        parts = [chips[it, j] for j in range(YS)]
        low_pair = compose(parts[0], parts[1])
        zown[it, 0] = compose(low_pair, compose(parts[2], parts[3]))

        h_copy_out = []

        def relay(to, level, valid):
            @pl.when(valid)
            def _():
                hvec[it, 1 + level] = apply(hvec[it, 0], zown[it, level])
                push(
                    hvec.at[it, 1 + level], hgot.at[it],
                    h_send.at[it, level], h_recv.at[it],
                    tm=jnp.minimum(z + to, nz - 1) * PLANE + inner,
                ).start()
            h_copy_out.append((to, level, valid))

        def receive(valid):
            @pl.when(valid)
            def _():
                push(
                    hgot.at[it], hgot.at[it], h_send.at[it, 0], h_recv.at[it],
                    tm=me,
                ).wait_recv()
                hvec[it, 0] = hgot[it]

        @pl.when(z == 0)
        def _():
            hvec[it, 0] = start

        z_out = []
        for k in range(ZROUNDS):
            d = 1 << k

            @pl.when(z >= d)
            def _():
                push(
                    zown.at[it, k], zgot.at[it, k], z_send.at[it, k], z_recv.at[it, k],
                    tm=(jnp.maximum(z - d, 0)) * PLANE + inner,
                ).start()

            z_out.append(d)
            if k > 0:
                receive((z >= d // 2) & (z < d))
            relay(d, k, z < d)

            @pl.when(z + d < nz)
            def _():
                push(
                    zown.at[it, k], zgot.at[it, k], z_send.at[it, k], z_recv.at[it, k],
                    tm=me,
                ).wait_recv()
                zown[it, k + 1] = compose(zown[it, k], zgot[it, k])

        wide = 1 << ZROUNDS
        known = 1 if ZROUNDS == 0 else wide // 2

        def inner_map():
            lead[0] = jnp.zeros((ROWS, H), F32)
            lead[1] = parts[0]
            lead[2] = low_pair
            lead[3] = compose(low_pair, parts[2])
            first_map = compose(
                lead[y], jnp.where(core == 1, theirs, jnp.zeros((ROWS, H), F32))
            )
            rest = [compose(first_map, heads[b]) for b in range(BLOCKS - 1)]
            acc[0] = first_map
            for b in range(BLOCKS - 1):
                acc[1 + b] = rest[b]

        @pl.when(z < known)
        def _():
            @pl.when(z + wide < nz)
            def _():
                hvec[it, 1 + ZROUNDS] = apply(hvec[it, 0], zown[it, ZROUNDS])
                push(
                    hvec.at[it, 1 + ZROUNDS], hgot.at[it],
                    h_send.at[it, ZROUNDS], h_recv.at[it],
                    tm=jnp.minimum(z + wide, nz - 1) * PLANE + inner,
                ).start()

        inner_map()
        receive(z >= known)
        relay(wide, ZROUNDS, (z >= known) & (z + wide < nz))

        entering = hvec[it, 0]
        at_device = apply(entering, acc[0])
        hbuf[0:8] = at_device
        for b in range(BLOCKS):
            head = at_device if b == 0 else apply(entering, acc[b])
            column = jnp.sum(eye * head[:1], axis=1, keepdims=True)
            rows = []
            for t in range(length):
                moved = jnp.sum(column * prefix[b, t, :H], axis=0, keepdims=True)
                rows.append(moved + prefix[b, t, H : H + 1] + head[:1])
            hbuf[8 + b * length : 8 + (b + 1) * length] = jnp.concatenate(rows, axis=0)
        current = hbuf[8 : 8 + steps]
        prev = hbuf[7 : 7 + steps]

        if it == 0:
            pl.semaphore_wait(reach.at[1], 2)
        for copy in [pair_copy] + chip_copies:
            copy.wait_send()
        for k, d in enumerate(z_out):
            @pl.when(z >= d)
            def _():
                push(
                    zown.at[it, k], zgot.at[it, k], z_send.at[it, k], z_recv.at[it, k],
                    tm=me,
                ).wait_send()
        for level in range(ZROUNDS + 1):
            d = 1 << level
            sent = (z + wide < nz) if level == ZROUNDS else (z < d)

            @pl.when(sent)
            def _():
                push(
                    hvec.at[it, 1 + level], hgot.at[it],
                    h_send.at[it, level], h_recv.at[it],
                    tm=me,
                ).wait_send()

    out_ref[...] = current
    stepped = cell(prev)[5]
    sums.append(jnp.sum(weight * (current - stepped) ** 2, axis=0, keepdims=True))
    total = jnp.concatenate(sums + [jnp.zeros((8 - ITERS, H), F32)], axis=0)

    def exchange(total, part, send, recv, mine, peers):
        part[mine] = total
        sent = []
        for j, (_, where) in enumerate(peers):
            copy = push(part.at[mine], part.at[mine], send.at[j], recv.at[mine], **where)
            copy.start()
            sent.append(copy)
        for j, (other, where) in enumerate(peers):
            push(
                part.at[other], part.at[other], send.at[j], recv.at[other], **where
            ).wait_recv()
        for copy in sent:
            copy.wait_send()
        total = part[0]
        for j in range(1, len(peers) + 1):
            total = total + part[j]
        return total

    total = exchange(
        total, part_a, a_send, a_recv, core, [(1 - core, {"tm": twin})]
    )
    total = exchange(
        total, part_b, b_send, b_recv, y * nx + col,
        [
            (
                (y + j) % YS * nx + (col + i) % nx,
                {"tm": along_y(j), "batch": (col + i) % nx},
            )
            for j, i in others
        ],
    )
    total = exchange(
        total, part_c, c_send, c_recv, z,
        [((z + j) % nz, {"tm": along_z(j)}) for j in far_z],
    )
    denom = nx * H * (steps * nz * PLANE + 1) / 2.0
    norms = jnp.sqrt(jnp.sum(total, axis=1, keepdims=True) / denom + 1e-06)
    for k in range(ITERS):
        norm_ref[k] = norms[k, 0]


def per_device(
    nz, nx, inputs, h_start, in_weight, rec_weight, update_bias, reset_bias,
    cand_bias, rec_bias,
):
    steps = inputs.shape[0]
    length = steps // BLOCKS
    vmem = pl.BlockSpec(memory_space=pltpu.VMEM)
    dma = pltpu.SemaphoreType.DMA
    states, norms = pl.pallas_call(
        functools.partial(kernel, nz, nx),
        out_shape=(
            jax.ShapeDtypeStruct((steps, H), F32),
            jax.ShapeDtypeStruct((ITERS,), F32),
        ),
        in_specs=[vmem] * 8,
        out_specs=(vmem, pl.BlockSpec(memory_space=pltpu.SMEM)),
        scratch_shapes=[
            pltpu.VMEM((steps, 3 * H), F32),
            pltpu.VMEM((4, steps, H), F32),
            pltpu.VMEM((steps, H), F32),
            pltpu.VMEM((BLOCKS, length, ROWS, H), F32),
            pltpu.VMEM((ITERS, ROWS, H), F32),
            pltpu.VMEM((ITERS, ROWS, H), F32),
            pltpu.VMEM((ITERS, YS, ROWS, H), F32),
            pltpu.VMEM((YS, ROWS, H), F32),
            pltpu.VMEM((BLOCKS, ROWS, H), F32),
            pltpu.VMEM((ITERS, ZROUNDS + 1, ROWS, H), F32),
            pltpu.VMEM((ITERS, max(ZROUNDS, 1), ROWS, H), F32),
            pltpu.VMEM((ITERS, ZROUNDS + 2, 8, H), F32),
            pltpu.VMEM((ITERS, 8, H), F32),
            pltpu.VMEM((8 + steps, H), F32),
            pltpu.VMEM((BLOCKS - 1, ROWS, H), F32),
            pltpu.VMEM((2, 8, H), F32),
            pltpu.VMEM((YS * nx, 8, H), F32),
            pltpu.VMEM((nz, 8, H), F32),
            pltpu.SemaphoreType.REGULAR((2,)),
            dma((ITERS,)), dma((ITERS,)),
            dma((ITERS, YS)), dma((ITERS, YS)),
            dma((ITERS, max(ZROUNDS, 1))), dma((ITERS, max(ZROUNDS, 1))),
            dma((ITERS, ZROUNDS + 1)), dma((ITERS,)),
            dma((1,)), dma((2,)),
            dma((YS * nx,)), dma((YS * nx,)),
            dma((nz,)), dma((nz,)),
        ],
        compiler_params=pltpu.CompilerParams(collective_id=0, has_side_effects=True),
        name="deer",
    )(
        inputs.reshape(steps, -1), h_start, in_weight, rec_weight,
        update_bias.reshape(1, H), reset_bias.reshape(1, H),
        cand_bias.reshape(1, H), rec_bias.reshape(1, H),
    )
    return states.reshape(steps, 1, H), norms


def solution(mesh):
    nz = mesh.shape["tm"] // PLANE
    nx = mesh.shape["batch"]
    in_specs = (P("tm", "batch", None), P("batch", None), P(), P(), P(), P(), P(), P())
    out_specs = (P("tm", "batch", None), P())
    return jax.shard_map(
        functools.partial(per_device, nz, nx), mesh=mesh, in_specs=in_specs,
        out_specs=out_specs, check_vma=False,
    )
```
